32 devices in a mesh: member: 2 (over x), tx: 4 (over y, core), ty: 4 (over z).
Axes of the slice: x: 2, y: 2, z: 4, core: 2. Of those that a mesh axis runs over, the one named last changes fastest.
Arguments:
- state: float32 [1024, 128, 128], P(('member', 'tx'), 'ty'), parts along dimension 0, may hold values from -6 to 6
- courant: bfloat16 [1024, 128, 128], P(('member', 'tx'), 'ty'), parts along dimension 0, may hold values from -0.3984375 to 0.3984375
- diffusion: float32 [1024, 128], P(('member', 'tx'), 'ty'), parts along dimension 0, may hold values from 0.02 to 0.2
- conv_mask: int32 [1024, 128], P(('member', 'tx'), 'ty'), parts along dimension 0, may hold values from 0 to 1, as said below
- w_in: bfloat16 [128, 1024], replicated, may hold values from -0.5 to 0.5
- w_hidden: bfloat16 [3, 1024, 1024], replicated, may hold values from -0.1875 to 0.1875
- w_out: bfloat16 [1024, 128], replicated, may hold values from -0.1875 to 0.1875
Outputs:
- state_out: float32 [1024, 128, 128], P(('member', 'tx'), 'ty'), parts along dimension 0
The draws below stay inside these ranges and needn't reach their ends.
There are 2 independent parts, one for each index of `member`. The reference program is written for one: setup_inputs(seed, part) draws one part's arguments, and reference() takes and returns one part's arrays. A program takes and returns all parts, laid end to end along the dimension named above; an argument that names none is the same for every part. Nothing has to cross between parts.
Inputs may be any that keep to these rules, and one draw needn't show every extreme that they name: `conv_mask`: A tile is one device's 128 x 32 columns. A tile's used blocks are ceil(its flagged columns / 32); at most 64, reached by some tile; over a member's tiles they sum to exactly 528.
All inputs are finite; a program needn't handle non-finite values.
Results may differ from the reference program's by a relative error of at most 0.00033.
Values may be sent and summed in bfloat16 or wider, within the bound.
A program may use at most 64 MiB of HBM per device.

```python
import math
import jax
import jax.numpy as jnp
from jax import lax

CLON = 128
CLAT = 32
LEV = 64
CH = 128
HID = 1024
LAYERS = 5
BLK = 32
NBLK = 64
MEAN = 33
NLON = 512
NLAT = 128
N_TX = 4
N_TY = 4


def tile_order(sub_key):
    return jax.random.permutation(sub_key, CLON * CLAT)


def draw_conv_mask(key, part):
    tile_count = N_TX * N_TY
    half_count = tile_count // 2
    key_pair = jax.random.fold_in(key, 3)
    key_perm = jax.random.fold_in(key, 5)
    key_trim = jax.random.fold_in(key, 7)
    key_rank = jax.random.fold_in(key, 11)
    first = jax.random.randint(key_pair, (half_count,), 2, 2 * MEAN - 1)
    first = first.at[0].set(NBLK)
    loads = jnp.concatenate([first, 2 * MEAN - first])
    loads = jax.random.permutation(key_perm, loads)
    trimmed = jax.random.randint(key_trim, (tile_count,), 0, BLK)
    trimmed = jnp.where(loads == NBLK, 0, trimmed)
    flagged = loads * BLK - trimmed
    ranks = jax.vmap(tile_order)(jax.random.split(key_rank, tile_count))
    marks = (ranks < flagged[:, None]).astype(jnp.int32)
    marks = marks.reshape(N_TX, N_TY, CLON, CLAT).transpose(0, 2, 1, 3)
    return marks.reshape(N_TX * CLON, N_TY * CLAT)


def block_scale(stream_key, extent, shards, least, largest):
    def one(position, shards_of):
        steps = jax.random.uniform(jax.random.fold_in(jax.random.fold_in(stream_key, 6), position), (shards_of,), jnp.float32, least / len(shards), largest / len(shards))
        return jnp.repeat(jnp.exp(steps), extent[position] // shards_of).reshape((-1,) + (1,) * (len(extent) - position - 1))

    loudness = one(*shards[0])
    for cut in shards[1:]:
        loudness = loudness * one(*cut)
    return loudness


def noise(own_key, shape, width, most, pieces=(), kind=jnp.bfloat16):
    result = jax.random.normal(own_key, shape, jnp.float32) * width
    if len(pieces) > 0:
        result = block_scale(own_key, shape, pieces, -0.22, 0.18) * result
    return jnp.clip(result, min=-most, max=most).astype(kind)


def setup_inputs(seed: int = 0, part: int = 0) -> dict:
    key_of = jax.random.split(jax.random.key(seed), 8)
    part_splits = jax.random.split(jax.random.fold_in(key_of[7], part), 8)
    return {
        "state": noise(part_splits[0], (NLON, NLAT, CH), 1.0, 6.0, ((0, 4), (1, 4)), jnp.float32),
        "courant": jnp.clip(jax.random.uniform(part_splits[1], (NLON, NLAT, CH), jnp.float32, -0.3984375, 0.3984375) * block_scale(part_splits[1], (NLON, NLAT, CH), ((0, 4), (1, 4)), -0.4, 0.0), -0.3984375, 0.3984375).astype(jnp.bfloat16),
        "diffusion": jnp.clip(jnp.exp(math.log(0.2) - 2.3025851 * jax.random.uniform(part_splits[2], (NLON, NLAT), jnp.float32) ** block_scale(part_splits[2], (NLON, NLAT), ((0, 4), (1, 4)), -0.2, 0.2)), 0.02, 0.2),
        "conv_mask": draw_conv_mask(jax.random.fold_in(jax.random.fold_in(key_of[7], part), 71), part),
        "w_in": noise(key_of[4], (CH, HID), CH ** -0.5, 0.5),
        "w_hidden": noise(key_of[5], (LAYERS - 2, HID, HID), HID ** -0.5, 0.1875),
        "w_out": noise(key_of[6], (HID, CH), HID ** -0.5, 0.1875),
    }


def advance(state, courant, diffusion):
    east = jnp.roll(state, -1, 0)
    west = jnp.roll(state, 1, 0)
    zero_line = jnp.zeros_like(state[:, :1])
    north = jnp.concatenate([state[:, 1:], zero_line], 1)
    south = jnp.concatenate([zero_line, state[:, :-1]], 1)
    wind = courant.astype(jnp.float32)
    along_lon = jnp.concatenate([wind[..., :LEV], wind[..., :LEV]], -1)
    along_lat = jnp.concatenate([wind[..., LEV:], wind[..., LEV:]], -1)
    laplace = east + west + north + south - 4.0 * state
    return state - 0.5 * along_lon * (east - west) - 0.5 * along_lat * (north - south) + diffusion[..., None] * laplace


def closure(inputs, w_in, w_hidden, w_out):
    hidden = jax.nn.silu(jnp.dot(inputs, w_in, preferred_element_type=jnp.float32)).astype(jnp.bfloat16)
    for layer_idx in range(w_hidden.shape[0]):
        hidden = jax.nn.silu(jnp.dot(hidden, w_hidden[layer_idx], preferred_element_type=jnp.float32)).astype(jnp.bfloat16)
    return jnp.dot(hidden, w_out, preferred_element_type=jnp.float32).astype(jnp.bfloat16)


def reference(state, courant, diffusion, conv_mask, w_in, w_hidden, w_out):
    advanced = advance(state, courant, diffusion)
    columns = NLON * NLAT
    capacity = N_TX * N_TY * MEAN * BLK
    flags = conv_mask.reshape(columns).astype(jnp.int32)
    ranks = (jnp.cumsum(flags) - 1).astype(jnp.int32)
    slot_pos = jnp.where(flags == 1, ranks, capacity).astype(jnp.int32)
    features = advanced.reshape(columns, CH).astype(jnp.bfloat16)
    packed = jnp.zeros((capacity, CH), jnp.bfloat16).at[slot_pos].set(features, mode="drop")
    groups = packed.reshape(N_TX * N_TY, MEAN * BLK, CH)
    tendency = lax.map(lambda group: closure(group, w_in, w_hidden, w_out), groups)
    tendency = tendency.reshape(capacity, CH)
    picked = tendency[jnp.minimum(slot_pos, capacity - 1)].astype(jnp.float32)
    added = jnp.where(flags[:, None] == 1, picked, jnp.float32(0.0))
    return (advanced.reshape(columns, CH) + added).reshape(NLON, NLAT, CH)
```

```python
import functools

import jax
import jax.numpy as jnp
from jax import lax
from jax.experimental import pallas as pl
from jax.experimental.pallas import tpu as pltpu
from jax.sharding import PartitionSpec as P

MESH = pl.DeviceIdType.MESH
PAD = 8
GRP = 8
TM = 512


def advance_kernel(ntx, nty, state_hbm, courant_ref, diffusion_ref, adv_ref, tile, lsem, ssem, rsem):
    lon, lat, ch = courant_ref.shape
    ix, iy = lax.axis_index("tx"), lax.axis_index("ty")
    east, west = lax.rem(ix + 1, ntx), lax.rem(ix + ntx - 1, ntx)
    has_n, has_s = iy < nty - 1, iy > 0

    load = pltpu.make_async_copy(state_hbm, tile.at[pl.ds(1, lon), pl.ds(PAD, lat)], lsem)
    load.start()
    barrier = pltpu.get_barrier_semaphore()
    pl.semaphore_signal(barrier, inc=1, device_id={"tx": east}, device_id_type=MESH)
    pl.semaphore_signal(barrier, inc=1, device_id={"tx": west}, device_id_type=MESH)

    @pl.when(has_n)
    def _():
        pl.semaphore_signal(barrier, inc=1, device_id={"ty": iy + 1}, device_id_type=MESH)

    @pl.when(has_s)
    def _():
        pl.semaphore_signal(barrier, inc=1, device_id={"ty": iy - 1}, device_id_type=MESH)

    @pl.when(jnp.logical_not(has_n))
    def _():
        tile[pl.ds(1, lon), pl.ds(PAD + lat, 1), :] = jnp.zeros((lon, 1, ch), jnp.float32)

    @pl.when(jnp.logical_not(has_s))
    def _():
        tile[pl.ds(1, lon), pl.ds(PAD - 1, 1), :] = jnp.zeros((lon, 1, ch), jnp.float32)

    pl.semaphore_wait(barrier, 2 + has_n.astype(jnp.int32) + has_s.astype(jnp.int32))

    def send(src, dst, k, dev):
        return pltpu.make_async_remote_copy(
            src_ref=src, dst_ref=dst, send_sem=ssem.at[k], recv_sem=rsem.at[k],
            device_id=dev, device_id_type=MESH)

    rows, cols = pl.ds(PAD, lat), pl.ds(1, lon)
    to_n = send(state_hbm.at[:, pl.ds(lat - 1, 1)], tile.at[cols, pl.ds(PAD - 1, 1)], 2, {"ty": iy + 1})
    to_s = send(state_hbm.at[:, pl.ds(0, 1)], tile.at[cols, pl.ds(PAD + lat, 1)], 3, {"ty": iy - 1})
    pl.when(has_n)(to_n.start)
    pl.when(has_s)(to_s.start)
    to_e = send(state_hbm.at[pl.ds(lon - 1, 1)], tile.at[pl.ds(0, 1), rows], 0, {"tx": east})
    to_w = send(state_hbm.at[pl.ds(0, 1)], tile.at[pl.ds(lon + 1, 1), rows], 1, {"tx": west})
    to_e.start()
    to_w.start()
    load.wait()
    to_e.wait()
    to_w.wait()

    @pl.when(has_n)
    def _():
        to_n.wait_send()
        to_s.wait_recv()

    @pl.when(has_s)
    def _():
        to_s.wait_send()
        to_n.wait_recv()

    half = ch // 2
    lane = lax.broadcasted_iota(jnp.int32, (GRP * lat, ch), 1)
    eye = (lax.broadcasted_iota(jnp.int32, (GRP, lat, lat), 1)
           == lax.broadcasted_iota(jnp.int32, (GRP, lat, lat), 2))

    @pl.loop(0, lon // GRP)
    def _(c):
        i0 = pl.multiple_of(c * GRP, GRP)

        def get(di, dj):
            return tile[pl.ds(i0 + 1 + di, GRP), pl.ds(PAD + dj, lat), :].reshape(GRP * lat, ch)

        mid, e, w, n, s = get(0, 0), get(1, 0), get(-1, 0), get(0, 1), get(0, -1)
        wind = courant_ref[pl.ds(i0, GRP)].reshape(GRP * lat, ch).astype(jnp.float32)
        turned = pltpu.roll(wind, half, 1)
        cx = jnp.where(lane < half, wind, turned)
        cy = jnp.where(lane < half, turned, wind)
        d8 = diffusion_ref[pl.ds(i0, GRP), :]
        dif = jnp.sum(jnp.where(eye, d8[:, None, :], 0.0), axis=-1, keepdims=True).reshape(GRP * lat, 1)
        laplace = e + w + n + s - 4.0 * mid
        adv_ref[pl.ds(pl.multiple_of(c * GRP * lat, GRP * lat), GRP * lat), :] = (
            mid - 0.5 * cx * (e - w) - 0.5 * cy * (n - s) + dif * laplace)


def closure_kernel(mask_ref, adv_hbm, win_hbm, whid_hbm, wout_hbm, out_hbm,
                   adv, win, whid, wout, packed, ha, hb, place, base_v, base_s, sems, osem):
    lon, lat = mask_ref.shape
    cols, ch = adv.shape
    wide = GRP * lat
    chunks = cols // wide
    span = wide + 16
    layers = whid.shape[0]
    cp_adv = pltpu.make_async_copy(adv_hbm, adv, sems.at[0])
    cp_in = pltpu.make_async_copy(win_hbm, win, sems.at[1])
    cp_out = pltpu.make_async_copy(wout_hbm, wout, sems.at[2])
    cp_hid = [pltpu.make_async_copy(whid_hbm.at[l], whid.at[l], sems.at[3 + l]) for l in range(layers)]
    cp_adv.start()
    cp_in.start()
    for cp in cp_hid:
        cp.start()
    cp_out.start()

    flags = mask_ref[...].astype(jnp.float32).astype(jnp.bfloat16)
    spread = (lax.broadcasted_iota(jnp.int32, (lat, wide), 1) % lat
              == lax.broadcasted_iota(jnp.int32, (lat, wide), 0)).astype(jnp.float32).astype(jnp.bfloat16)
    rep = jnp.dot(flags, spread, preferred_element_type=jnp.float32)
    keep = (lax.broadcasted_iota(jnp.int32, (lon, wide), 1) // lat
            == lax.broadcasted_iota(jnp.int32, (lon, wide), 0) % GRP)
    rows = jnp.sum(jnp.where(keep, rep, 0.0).reshape(chunks, GRP, wide), axis=1)
    upper = (lax.broadcasted_iota(jnp.int32, (wide, wide), 0)
             < lax.broadcasted_iota(jnp.int32, (wide, wide), 1)).astype(jnp.float32).astype(jnp.bfloat16)
    rank = jnp.dot(rows.astype(jnp.bfloat16), upper, preferred_element_type=jnp.float32)
    total = jnp.sum(rows, axis=1, keepdims=True)
    lower = (lax.broadcasted_iota(jnp.int32, (chunks, chunks), 1)
             < lax.broadcasted_iota(jnp.int32, (chunks, chunks), 0)).astype(jnp.float32).astype(jnp.bfloat16)
    base = jnp.dot(lower, jnp.broadcast_to(total, (chunks, 128)).astype(jnp.bfloat16),
                   preferred_element_type=jnp.float32)
    base_i = base.astype(jnp.int32)
    base_v[...] = base_i
    cp_base = pltpu.make_async_copy(base_v, base_s, sems.at[3 + layers])
    cp_base.start()
    rest = (base_i - (base_i // 16) * 16)[:, :1].astype(jnp.float32)
    place[...] = jnp.where(rows > 0.5, rank + rest, -1.0)
    packed[...] = jnp.zeros_like(packed)
    cp_base.wait()
    cp_adv.wait()

    sub = lax.broadcasted_iota(jnp.int32, (span, wide), 0).astype(jnp.float32)

    def onehot(c):
        row = place[pl.ds(c, 1), :]
        return jnp.where(sub == row, 1.0, 0.0).astype(jnp.bfloat16)

    def start_of(c):
        return pl.multiple_of((base_s[c, 0] // 16) * 16, 16)

    for c in range(chunks):
        b = start_of(c)
        feats = adv[pl.ds(c * wide, wide), :].astype(jnp.bfloat16)
        res = jnp.dot(onehot(c), feats, preferred_element_type=jnp.float32).astype(jnp.bfloat16)
        packed[pl.ds(b, 16), :] = packed[pl.ds(b, 16), :] + res[:16]
        packed[pl.ds(pl.multiple_of(b + 16, 16), wide), :] = res[16:]

    cp_in.wait()
    for cp in cp_hid:
        cp.wait()
    cp_out.wait()

    def silu(v):
        hv = 0.5 * v
        return (hv + hv * jnp.tanh(hv)).astype(jnp.bfloat16)

    hid = win.shape[1]
    step = 256

    @pl.loop(0, cols // 2 // TM)
    def _(t):
        r = pl.ds(pl.multiple_of(t * TM, TM), TM)
        x = packed[r, :]
        for n in range(0, hid, step):
            ha[:, n:n + step] = silu(jnp.dot(x, win[:, n:n + step], preferred_element_type=jnp.float32))
        src, dst = ha, hb
        for l in range(layers):
            for n in range(0, hid, step):
                dst[:, n:n + step] = silu(
                    jnp.dot(src[...], whid[l, :, n:n + step], preferred_element_type=jnp.float32))
            src, dst = dst, src
        packed[r, :] = jnp.dot(src[...], wout[...], preferred_element_type=jnp.float32).astype(jnp.bfloat16)

    outs = []
    for c in range(chunks):
        b = start_of(c)
        got = lax.dot_general(onehot(c), packed[pl.ds(b, span), :], (((0,), (0,)), ((), ())),
                              preferred_element_type=jnp.float32)
        r = pl.ds(c * wide, wide)
        adv[r, :] = adv[r, :] + got
        cp = pltpu.make_async_copy(adv.at[r, :], out_hbm.at[r, :], osem.at[c])
        cp.start()
        outs.append(cp)
    for cp in outs:
        cp.wait()


def local(ntx, nty, state, courant, diffusion, conv_mask, w_in, w_hidden, w_out):
    lon, lat, ch = state.shape
    cols = lon * lat
    hid = w_in.shape[1]
    layers = w_hidden.shape[0]
    wide = GRP * lat
    chunks = cols // wide
    vmem = pl.BlockSpec(memory_space=pltpu.VMEM)
    hbm = pl.BlockSpec(memory_space=pl.ANY)
    adv = pl.pallas_call(
        functools.partial(advance_kernel, ntx, nty),
        out_shape=jax.ShapeDtypeStruct((cols, ch), jnp.float32),
        in_specs=[hbm, vmem, vmem],
        out_specs=vmem,
        scratch_shapes=[
            pltpu.VMEM((lon + 2, lat + 2 * PAD, ch), jnp.float32),
            pltpu.SemaphoreType.DMA,
            pltpu.SemaphoreType.DMA((4,)),
            pltpu.SemaphoreType.DMA((4,)),
        ],
        compiler_params=pltpu.CompilerParams(collective_id=0, has_side_effects=True,
                                             vmem_limit_bytes=16 << 20),
        name="advance",
    )(state, courant, diffusion)
    out = pl.pallas_call(
        closure_kernel,
        out_shape=jax.ShapeDtypeStruct((cols, ch), jnp.float32),
        in_specs=[vmem, hbm, hbm, hbm, hbm],
        out_specs=hbm,
        scratch_shapes=[
            pltpu.VMEM((cols, ch), jnp.float32),
            pltpu.VMEM(w_in.shape, jnp.bfloat16),
            pltpu.VMEM(w_hidden.shape, jnp.bfloat16),
            pltpu.VMEM(w_out.shape, jnp.bfloat16),
            pltpu.VMEM((cols // 2 + wide + 32, ch), jnp.bfloat16),
            pltpu.VMEM((TM, hid), jnp.bfloat16),
            pltpu.VMEM((TM, hid), jnp.bfloat16),
            pltpu.VMEM((chunks, wide), jnp.float32),
            pltpu.VMEM((chunks, 128), jnp.int32),
            pltpu.SMEM((chunks, 128), jnp.int32),
            pltpu.SemaphoreType.DMA((4 + layers,)),
            pltpu.SemaphoreType.DMA((chunks,)),
        ],
        compiler_params=pltpu.CompilerParams(vmem_limit_bytes=40 << 20),
        name="closure",
    )(conv_mask, adv, w_in, w_hidden, w_out)
    return out.reshape(lon, lat, ch)


def solution(mesh):
    spec = P(("member", "tx"), "ty", None)
    flat = P(("member", "tx"), "ty")
    return jax.shard_map(
        functools.partial(local, mesh.shape["tx"], mesh.shape["ty"]),
        mesh=mesh,
        in_specs=(spec, spec, flat, flat, P(), P(), P()),
        out_specs=spec,
        check_vma=False,
    )
```

```python
import functools

import jax
import jax.numpy as jnp
from jax import lax
from jax.experimental import pallas as pl
from jax.experimental.pallas import tpu as pltpu
from jax.sharding import PartitionSpec as P

MESH = pl.DeviceIdType.MESH
PAD = 8
PIECES = 4
GRP = 8
ROOM = (61 << 20) + (3 << 18)
TM = 1024


def advance_kernel(ntx, nty, state_hbm, courant_hbm, diffusion_ref, adv_ref, tile, wind_v, halo_n, halo_s,
                   halo_e, halo_w, coef_n, coef_s, lsem, csem, ssem, rsem):
    lon, lat, ch = wind_v.shape
    ix, iy = lax.axis_index("tx"), lax.axis_index("ty")
    east, west = lax.rem(ix + 1, ntx), lax.rem(ix + ntx - 1, ntx)
    has_n, has_s = iy < nty - 1, iy > 0
    part = lon // PIECES

    barrier = pltpu.get_barrier_semaphore()
    pl.semaphore_signal(barrier, inc=1, device_id={"tx": east}, device_id_type=MESH)
    pl.semaphore_signal(barrier, inc=1, device_id={"tx": west}, device_id_type=MESH)

    @pl.when(has_n)
    def _():
        pl.semaphore_signal(barrier, inc=1, device_id={"ty": iy + 1}, device_id_type=MESH)

    @pl.when(has_s)
    def _():
        pl.semaphore_signal(barrier, inc=1, device_id={"ty": iy - 1}, device_id_type=MESH)

    loads = []
    for k in range(PIECES):
        loads.append((
            pltpu.make_async_copy(state_hbm.at[pl.ds(k * part, part)],
                                  tile.at[pl.ds(1 + k * part, part), pl.ds(PAD, lat)], lsem.at[k]),
            pltpu.make_async_copy(courant_hbm.at[pl.ds(k * part, part)],
                                  wind_v.at[pl.ds(k * part, part)], csem.at[k])))
        for cp in loads[-1]:
            cp.start()

    @pl.when(jnp.logical_not(has_n))
    def _():
        halo_n[...] = jnp.zeros_like(halo_n)

    @pl.when(jnp.logical_not(has_s))
    def _():
        halo_s[...] = jnp.zeros_like(halo_s)

    edge = jnp.zeros((lon, 1, ch), jnp.float32)
    tile[pl.ds(1, lon), pl.ds(PAD - 1, 1), :] = edge
    tile[pl.ds(1, lon), pl.ds(PAD + lat, 1), :] = edge
    tile[pl.ds(0, 1), pl.ds(PAD, lat), :] = jnp.zeros((1, lat, ch), jnp.float32)
    tile[pl.ds(lon + 1, 1), pl.ds(PAD, lat), :] = jnp.zeros((1, lat, ch), jnp.float32)

    pl.semaphore_wait(barrier, 2 + has_n.astype(jnp.int32) + has_s.astype(jnp.int32))

    def send(src, dst, k, dev):
        return pltpu.make_async_remote_copy(
            src_ref=src, dst_ref=dst, send_sem=ssem.at[k], recv_sem=rsem.at[k],
            device_id=dev, device_id_type=MESH)

    to_n = send(state_hbm.at[:, pl.ds(lat - 1, 1)], halo_s, 2, {"ty": iy + 1})
    to_s = send(state_hbm.at[:, pl.ds(0, 1)], halo_n, 3, {"ty": iy - 1})
    to_e = send(state_hbm.at[pl.ds(lon - 1, 1)], halo_w, 0, {"tx": east})
    to_w = send(state_hbm.at[pl.ds(0, 1)], halo_e, 1, {"tx": west})
    pl.when(has_n)(to_n.start)
    pl.when(has_s)(to_s.start)
    to_e.start()
    to_w.start()

    half = ch // 2
    shape = (GRP, lat, ch)
    lane2 = lax.broadcasted_iota(jnp.int32, (GRP * lat, ch), 1)
    lane3 = lax.broadcasted_iota(jnp.int32, shape, 2)
    row3 = lax.broadcasted_iota(jnp.int32, shape, 0)

    def fields(i0):
        wind = wind_v[pl.ds(i0, GRP)].reshape(GRP * lat, ch).astype(jnp.float32) * 0.5
        turned = pltpu.roll(wind, half, 1)
        cx = jnp.where(lane2 < half, wind, turned).reshape(shape)
        cy = jnp.where(lane2 < half, turned, wind).reshape(shape)
        pick = jnp.where(lane3 == row3 + i0, diffusion_ref[...][None], 0.0)
        return cx, cy, jnp.sum(pick, axis=-1, keepdims=True)

    for k in range(PIECES):
        for piece in ([0, 1] if k == 0 else [k + 1]):
            if piece < PIECES:
                for cp in loads[piece]:
                    cp.wait()

        @pl.loop(k * part // GRP, (k + 1) * part // GRP)
        def _(c):
            i0 = pl.multiple_of(c * GRP, GRP)

            def get(di, dj):
                return tile[pl.ds(i0 + 1 + di, GRP), pl.ds(PAD + dj, lat), :]

            mid, e, w, n, s = get(0, 0), get(1, 0), get(-1, 0), get(0, 1), get(0, -1)
            cx, cy, dif = fields(i0)
            coef_n[pl.ds(i0, GRP)] = (dif - cy)[:, lat - 8:]
            coef_s[pl.ds(i0, GRP)] = (dif + cy)[:, :8]
            laplace = e + w + n + s - 4.0 * mid
            adv_ref[pl.ds(i0, GRP)] = mid - cx * (e - w) - cy * (n - s) + dif * laplace

    to_e.wait()
    to_w.wait()

    @pl.when(has_n)
    def _():
        to_n.wait_send()
        to_s.wait_recv()

    @pl.when(has_s)
    def _():
        to_s.wait_send()
        to_n.wait_recv()

    cx, _, dif = fields(0)
    adv_ref[pl.ds(0, 1)] = adv_ref[pl.ds(0, 1)] + ((dif + cx)[:1]) * halo_w[...]
    cx, _, dif = fields(lon - GRP)
    adv_ref[pl.ds(lon - 1, 1)] = adv_ref[pl.ds(lon - 1, 1)] + ((dif - cx)[GRP - 1:]) * halo_e[...]
    sub = lax.broadcasted_iota(jnp.int32, (2 * GRP, 8, ch), 1)

    @pl.loop(0, lon // (2 * GRP))
    def _(c):
        r = pl.ds(pl.multiple_of(c * 2 * GRP, 2 * GRP), 2 * GRP)
        lo, hi = pl.ds(0, 8), pl.ds(lat - 8, 8)
        adv_ref[r, lo, :] = adv_ref[r, lo, :] + jnp.where(sub == 0, coef_s[r] * halo_s[r], 0.0)
        adv_ref[r, hi, :] = adv_ref[r, hi, :] + jnp.where(sub == 7, coef_n[r] * halo_n[r], 0.0)


def closure_kernel(mask_ref, adv, win_hbm, whid_hbm, wout_hbm, out_hbm,
                   done, win, whid, wout, packed, ha, hb, place, base_v, base_s, sems, osem):
    lat, lon = mask_ref.shape
    cols, ch = done.shape
    wide = GRP * lat
    chunks = cols // wide
    span = wide + 16
    layers = whid.shape[0]
    cp_in = pltpu.make_async_copy(win_hbm, win, sems.at[1])
    cp_out = pltpu.make_async_copy(wout_hbm, wout, sems.at[2])
    cp_hid = [pltpu.make_async_copy(whid_hbm.at[l], whid.at[l], sems.at[3 + l]) for l in range(layers)]
    cp_in.start()
    for cp in cp_hid:
        cp.start()
    cp_out.start()

    flags = mask_ref[...].astype(jnp.float32).astype(jnp.bfloat16)
    spread = (lax.broadcasted_iota(jnp.int32, (lat, wide), 1) % lat
              == lax.broadcasted_iota(jnp.int32, (lat, wide), 0)).astype(jnp.float32).astype(jnp.bfloat16)
    rep = lax.dot_general(flags, spread, (((0,), (0,)), ((), ())), preferred_element_type=jnp.float32)
    keep = (lax.broadcasted_iota(jnp.int32, (lon, wide), 1) // lat
            == lax.broadcasted_iota(jnp.int32, (lon, wide), 0) % GRP)
    rows = jnp.sum(jnp.where(keep, rep, 0.0).reshape(chunks, GRP, wide), axis=1)
    upper = (lax.broadcasted_iota(jnp.int32, (wide, wide), 0)
             < lax.broadcasted_iota(jnp.int32, (wide, wide), 1)).astype(jnp.float32).astype(jnp.bfloat16)
    rank = jnp.dot(rows.astype(jnp.bfloat16), upper, preferred_element_type=jnp.float32)
    total = jnp.sum(rows, axis=1, keepdims=True)
    lower = (lax.broadcasted_iota(jnp.int32, (chunks, chunks), 1)
             < lax.broadcasted_iota(jnp.int32, (chunks, chunks), 0)).astype(jnp.float32).astype(jnp.bfloat16)
    base = jnp.dot(lower, jnp.broadcast_to(total, (chunks, 128)).astype(jnp.bfloat16),
                   preferred_element_type=jnp.float32)
    base_i = base.astype(jnp.int32)
    base_v[...] = base_i
    cp_base = pltpu.make_async_copy(base_v, base_s, sems.at[3 + layers])
    cp_base.start()
    rest = (base_i - (base_i // 16) * 16)[:, :1].astype(jnp.float32)
    place[...] = jnp.where(rows > 0.5, rank + rest, -1.0)
    packed[...] = jnp.zeros_like(packed)
    cp_base.wait()

    sub = lax.broadcasted_iota(jnp.int32, (span, wide), 0).astype(jnp.float32)

    def onehot(c):
        row = place[pl.ds(c, 1), :]
        return jnp.where(sub == row, 1.0, 0.0).astype(jnp.bfloat16)

    def start_of(c):
        return pl.multiple_of((base_s[c, 0] // 16) * 16, 16)

    for c in range(chunks):
        b = start_of(c)
        feats = adv[pl.ds(c * GRP, GRP)].reshape(wide, ch).astype(jnp.bfloat16)
        res = jnp.dot(onehot(c), feats, preferred_element_type=jnp.float32).astype(jnp.bfloat16)
        packed[pl.ds(b, 16), :] = packed[pl.ds(b, 16), :] + res[:16]
        packed[pl.ds(pl.multiple_of(b + 16, 16), wide), :] = res[16:]

    cp_in.wait()

    def silu(v):
        hv = 0.5 * v
        return (hv + hv * jnp.tanh(hv)).astype(jnp.bfloat16)

    hid = win.shape[1]
    step = 256

    @pl.loop(0, cols // 2 // TM)
    def _(t):
        r = pl.ds(pl.multiple_of(t * TM, TM), TM)
        x = packed[r, :]
        for n in range(0, hid, step):
            ha[:, n:n + step] = silu(jnp.dot(x, win[:, n:n + step], preferred_element_type=jnp.float32))
        src, dst = ha, hb
        for l in range(layers):
            pl.when(t == 0)(cp_hid[l].wait)
            for n in range(0, hid, step):
                dst[:, n:n + step] = silu(
                    jnp.dot(src[...], whid[l, :, n:n + step], preferred_element_type=jnp.float32))
            src, dst = dst, src
        pl.when(t == 0)(cp_out.wait)
        packed[r, :] = jnp.dot(src[...], wout[...], preferred_element_type=jnp.float32).astype(jnp.bfloat16)

    outs = []
    for c in range(chunks):
        b = start_of(c)
        got = lax.dot_general(onehot(c), packed[pl.ds(b, span), :], (((0,), (0,)), ((), ())),
                              preferred_element_type=jnp.float32)
        r = pl.ds(c * wide, wide)
        done[r, :] = adv[pl.ds(c * GRP, GRP)].reshape(wide, ch) + got
        cp = pltpu.make_async_copy(done.at[r, :], out_hbm.at[r, :], osem.at[c])
        cp.start()
        outs.append(cp)
    for cp in outs:
        cp.wait()


def local(ntx, nty, state, courant, diffusion, conv_mask, w_in, w_hidden, w_out):
    lon, lat, ch = state.shape
    cols = lon * lat
    hid = w_in.shape[1]
    layers = w_hidden.shape[0]
    wide = GRP * lat
    chunks = cols // wide
    vmem = pl.BlockSpec(memory_space=pltpu.VMEM)
    hbm = pl.BlockSpec(memory_space=pltpu.MemorySpace.HBM)
    adv = pl.pallas_call(
        functools.partial(advance_kernel, ntx, nty),
        out_shape=jax.ShapeDtypeStruct((lon, lat, ch), jnp.float32),
        in_specs=[hbm, hbm, vmem],
        out_specs=vmem,
        scratch_shapes=[
            pltpu.VMEM((lon + 2, lat + 2 * PAD, ch), jnp.float32),
            pltpu.VMEM((lon, lat, ch), jnp.bfloat16),
            pltpu.VMEM((lon, 1, ch), jnp.float32),
            pltpu.VMEM((lon, 1, ch), jnp.float32),
            pltpu.VMEM((1, lat, ch), jnp.float32),
            pltpu.VMEM((1, lat, ch), jnp.float32),
            pltpu.VMEM((lon, 8, ch), jnp.float32),
            pltpu.VMEM((lon, 8, ch), jnp.float32),
            pltpu.SemaphoreType.DMA((PIECES,)),
            pltpu.SemaphoreType.DMA((PIECES,)),
            pltpu.SemaphoreType.DMA((4,)),
            pltpu.SemaphoreType.DMA((4,)),
        ],
        compiler_params=pltpu.CompilerParams(collective_id=0, has_side_effects=True,
                                             vmem_limit_bytes=ROOM),
        name="advance",
    )(state, courant, diffusion.T)
    out = pl.pallas_call(
        closure_kernel,
        out_shape=jax.ShapeDtypeStruct((cols, ch), jnp.float32),
        in_specs=[vmem, vmem, hbm, hbm, hbm],
        out_specs=hbm,
        scratch_shapes=[
            pltpu.VMEM((cols, ch), jnp.float32),
            pltpu.VMEM(w_in.shape, jnp.bfloat16),
            pltpu.VMEM(w_hidden.shape, jnp.bfloat16),
            pltpu.VMEM(w_out.shape, jnp.bfloat16),
            pltpu.VMEM((cols // 2 + wide + 32, ch), jnp.bfloat16),
            pltpu.VMEM((TM, hid), jnp.bfloat16),
            pltpu.VMEM((TM, hid), jnp.bfloat16),
            pltpu.VMEM((chunks, wide), jnp.float32),
            pltpu.VMEM((chunks, 128), jnp.int32),
            pltpu.SMEM((chunks, 128), jnp.int32),
            pltpu.SemaphoreType.DMA((4 + layers,)),
            pltpu.SemaphoreType.DMA((chunks,)),
        ],
        compiler_params=pltpu.CompilerParams(vmem_limit_bytes=ROOM),
        name="closure",
    )(conv_mask.T, adv, w_in, w_hidden, w_out)
    return out.reshape(lon, lat, ch)


def solution(mesh):
    spec = P(("member", "tx"), "ty", None)
    flat = P(("member", "tx"), "ty")
    return jax.shard_map(
        functools.partial(local, mesh.shape["tx"], mesh.shape["ty"]),
        mesh=mesh,
        in_specs=(spec, spec, flat, flat, P(), P(), P()),
        out_specs=spec,
        check_vma=False,
    )
```

```python
import functools

import jax
import jax.numpy as jnp
from jax import lax
from jax.experimental import pallas as pl
from jax.experimental.pallas import tpu as pltpu
from jax.sharding import PartitionSpec as P

MESH = pl.DeviceIdType.MESH
PAD = 8
PIECES = 4
GRP = 8
ROOM = 55 << 20
TM = 1024


def advance_kernel(ntx, nty, state_hbm, courant_hbm, diffusion_ref, win_hbm, whid_hbm, wout_hbm,
                   adv_ref, win_ref, whid_ref, wout_ref, tile, wind_v, halo_n, halo_s,
                   halo_e, halo_w, coef_n, coef_s, lsem, csem, wsem, ssem, rsem):
    lon, lat, ch = wind_v.shape
    ix, iy = lax.axis_index("tx"), lax.axis_index("ty")
    east, west = lax.rem(ix + 1, ntx), lax.rem(ix + ntx - 1, ntx)
    has_n, has_s = iy < nty - 1, iy > 0
    part = lon // PIECES

    barrier = pltpu.get_barrier_semaphore()
    pl.semaphore_signal(barrier, inc=1, device_id={"tx": east}, device_id_type=MESH)
    pl.semaphore_signal(barrier, inc=1, device_id={"tx": west}, device_id_type=MESH)

    @pl.when(has_n)
    def _():
        pl.semaphore_signal(barrier, inc=1, device_id={"ty": iy + 1}, device_id_type=MESH)

    @pl.when(has_s)
    def _():
        pl.semaphore_signal(barrier, inc=1, device_id={"ty": iy - 1}, device_id_type=MESH)

    loads = []
    for k in range(PIECES):
        loads.append((
            pltpu.make_async_copy(state_hbm.at[pl.ds(k * part, part)],
                                  tile.at[pl.ds(1 + k * part, part), pl.ds(PAD, lat)], lsem.at[k]),
            pltpu.make_async_copy(courant_hbm.at[pl.ds(k * part, part)],
                                  wind_v.at[pl.ds(k * part, part)], csem.at[k])))
        for cp in loads[-1]:
            cp.start()
    weights = [pltpu.make_async_copy(src, dst, wsem.at[k]) for k, (src, dst) in enumerate(
        ((win_hbm, win_ref), (whid_hbm, whid_ref), (wout_hbm, wout_ref)))]
    for cp in weights:
        cp.start()

    @pl.when(jnp.logical_not(has_n))
    def _():
        halo_n[...] = jnp.zeros_like(halo_n)

    @pl.when(jnp.logical_not(has_s))
    def _():
        halo_s[...] = jnp.zeros_like(halo_s)

    edge = jnp.zeros((lon, 1, ch), jnp.float32)
    tile[pl.ds(1, lon), pl.ds(PAD - 1, 1), :] = edge
    tile[pl.ds(1, lon), pl.ds(PAD + lat, 1), :] = edge
    tile[pl.ds(0, 1), pl.ds(PAD, lat), :] = jnp.zeros((1, lat, ch), jnp.float32)
    tile[pl.ds(lon + 1, 1), pl.ds(PAD, lat), :] = jnp.zeros((1, lat, ch), jnp.float32)

    pl.semaphore_wait(barrier, 2 + has_n.astype(jnp.int32) + has_s.astype(jnp.int32))

    def send(src, dst, k, dev):
        return pltpu.make_async_remote_copy(
            src_ref=src, dst_ref=dst, send_sem=ssem.at[k], recv_sem=rsem.at[k],
            device_id=dev, device_id_type=MESH)

    to_n = send(state_hbm.at[:, pl.ds(lat - 1, 1)], halo_s, 2, {"ty": iy + 1})
    to_s = send(state_hbm.at[:, pl.ds(0, 1)], halo_n, 3, {"ty": iy - 1})
    to_e = send(state_hbm.at[pl.ds(lon - 1, 1)], halo_w, 0, {"tx": east})
    to_w = send(state_hbm.at[pl.ds(0, 1)], halo_e, 1, {"tx": west})
    pl.when(has_n)(to_n.start)
    pl.when(has_s)(to_s.start)
    to_e.start()
    to_w.start()

    half = ch // 2
    shape = (GRP, lat, ch)
    lane2 = lax.broadcasted_iota(jnp.int32, (GRP * lat, ch), 1)
    lane3 = lax.broadcasted_iota(jnp.int32, shape, 2)
    row3 = lax.broadcasted_iota(jnp.int32, shape, 0)

    def fields(i0):
        wind = wind_v[pl.ds(i0, GRP)].reshape(GRP * lat, ch).astype(jnp.float32) * 0.5
        turned = pltpu.roll(wind, half, 1)
        cx = jnp.where(lane2 < half, wind, turned).reshape(shape)
        cy = jnp.where(lane2 < half, turned, wind).reshape(shape)
        pick = jnp.where(lane3 == row3 + i0, diffusion_ref[...][None], 0.0)
        return cx, cy, jnp.sum(pick, axis=-1, keepdims=True)

    for k in range(PIECES):
        for piece in ([0, 1] if k == 0 else [k + 1]):
            if piece < PIECES:
                for cp in loads[piece]:
                    cp.wait()

        @pl.loop(k * part // GRP, (k + 1) * part // GRP)
        def _(c):
            i0 = pl.multiple_of(c * GRP, GRP)

            def get(di, dj):
                return tile[pl.ds(i0 + 1 + di, GRP), pl.ds(PAD + dj, lat), :]

            mid, e, w, n, s = get(0, 0), get(1, 0), get(-1, 0), get(0, 1), get(0, -1)
            cx, cy, dif = fields(i0)
            coef_n[pl.ds(i0, GRP)] = (dif - cy)[:, lat - 8:]
            coef_s[pl.ds(i0, GRP)] = (dif + cy)[:, :8]
            laplace = e + w + n + s - 4.0 * mid
            adv_ref[pl.ds(i0, GRP)] = mid - cx * (e - w) - cy * (n - s) + dif * laplace

    to_e.wait()
    to_w.wait()

    @pl.when(has_n)
    def _():
        to_n.wait_send()
        to_s.wait_recv()

    @pl.when(has_s)
    def _():
        to_s.wait_send()
        to_n.wait_recv()

    cx, _, dif = fields(0)
    adv_ref[pl.ds(0, 1)] = adv_ref[pl.ds(0, 1)] + ((dif + cx)[:1]) * halo_w[...]
    cx, _, dif = fields(lon - GRP)
    adv_ref[pl.ds(lon - 1, 1)] = adv_ref[pl.ds(lon - 1, 1)] + ((dif - cx)[GRP - 1:]) * halo_e[...]
    sub = lax.broadcasted_iota(jnp.int32, (2 * GRP, 8, ch), 1)

    @pl.loop(0, lon // (2 * GRP))
    def _(c):
        r = pl.ds(pl.multiple_of(c * 2 * GRP, 2 * GRP), 2 * GRP)
        lo, hi = pl.ds(0, 8), pl.ds(lat - 8, 8)
        adv_ref[r, lo, :] = adv_ref[r, lo, :] + jnp.where(sub == 0, coef_s[r] * halo_s[r], 0.0)
        adv_ref[r, hi, :] = adv_ref[r, hi, :] + jnp.where(sub == 7, coef_n[r] * halo_n[r], 0.0)

    for cp in weights:
        cp.wait()


def closure_kernel(mask_ref, adv, win, whid, wout, out_hbm, done, packed, ha, hb, place, base_v, base_s, bsem, osem):
    lat, lon = mask_ref.shape
    cols, ch = done.shape
    wide = GRP * lat
    chunks = cols // wide
    span = wide + 16
    layers = whid.shape[0]
    flags = mask_ref[...].astype(jnp.float32).astype(jnp.bfloat16)
    spread = (lax.broadcasted_iota(jnp.int32, (lat, wide), 1) % lat
              == lax.broadcasted_iota(jnp.int32, (lat, wide), 0)).astype(jnp.float32).astype(jnp.bfloat16)
    rep = lax.dot_general(flags, spread, (((0,), (0,)), ((), ())), preferred_element_type=jnp.float32)
    keep = (lax.broadcasted_iota(jnp.int32, (lon, wide), 1) // lat
            == lax.broadcasted_iota(jnp.int32, (lon, wide), 0) % GRP)
    rows = jnp.sum(jnp.where(keep, rep, 0.0).reshape(chunks, GRP, wide), axis=1)
    upper = (lax.broadcasted_iota(jnp.int32, (wide, wide), 0)
             < lax.broadcasted_iota(jnp.int32, (wide, wide), 1)).astype(jnp.float32).astype(jnp.bfloat16)
    rank = jnp.dot(rows.astype(jnp.bfloat16), upper, preferred_element_type=jnp.float32)
    total = jnp.sum(rows, axis=1, keepdims=True)
    lower = (lax.broadcasted_iota(jnp.int32, (chunks, chunks), 1)
             < lax.broadcasted_iota(jnp.int32, (chunks, chunks), 0)).astype(jnp.float32).astype(jnp.bfloat16)
    base = jnp.dot(lower, jnp.broadcast_to(total, (chunks, 128)).astype(jnp.bfloat16),
                   preferred_element_type=jnp.float32)
    base_i = base.astype(jnp.int32)
    base_v[...] = base_i
    cp_base = pltpu.make_async_copy(base_v, base_s, bsem)
    cp_base.start()
    rest = (base_i - (base_i // 16) * 16)[:, :1].astype(jnp.float32)
    place[...] = jnp.where(rows > 0.5, rank + rest, -1.0)
    packed[...] = jnp.zeros_like(packed)
    cp_base.wait()

    sub = lax.broadcasted_iota(jnp.int32, (span, wide), 0).astype(jnp.float32)

    def onehot(c):
        row = place[pl.ds(c, 1), :]
        return jnp.where(sub == row, 1.0, 0.0).astype(jnp.bfloat16)

    def start_of(c):
        return pl.multiple_of((base_s[c, 0] // 16) * 16, 16)

    for c in range(chunks):
        b = start_of(c)
        feats = adv[pl.ds(c * GRP, GRP)].reshape(wide, ch).astype(jnp.bfloat16)
        res = jnp.dot(onehot(c), feats, preferred_element_type=jnp.float32).astype(jnp.bfloat16)
        packed[pl.ds(b, 16), :] = packed[pl.ds(b, 16), :] + res[:16]
        packed[pl.ds(pl.multiple_of(b + 16, 16), wide), :] = res[16:]

    def silu(v):
        hv = 0.5 * v
        return (hv + hv * jnp.tanh(hv)).astype(jnp.bfloat16)

    hid = win.shape[1]
    step = 256

    @pl.loop(0, cols // 2 // TM)
    def _(t):
        r = pl.ds(pl.multiple_of(t * TM, TM), TM)
        x = packed[r, :]
        for n in range(0, hid, step):
            ha[:, n:n + step] = silu(jnp.dot(x, win[:, n:n + step], preferred_element_type=jnp.float32))
        src, dst = ha, hb
        for l in range(layers):
            for n in range(0, hid, step):
                dst[:, n:n + step] = silu(
                    jnp.dot(src[...], whid[l, :, n:n + step], preferred_element_type=jnp.float32))
            src, dst = dst, src
        packed[r, :] = jnp.dot(src[...], wout[...], preferred_element_type=jnp.float32).astype(jnp.bfloat16)

    outs = []
    for c in range(chunks):
        b = start_of(c)
        got = lax.dot_general(onehot(c), packed[pl.ds(b, span), :], (((0,), (0,)), ((), ())),
                              preferred_element_type=jnp.float32)
        r = pl.ds(c * wide, wide)
        done[r, :] = adv[pl.ds(c * GRP, GRP)].reshape(wide, ch) + got
        cp = pltpu.make_async_copy(done.at[r, :], out_hbm.at[r, :], osem.at[c])
        cp.start()
        outs.append(cp)
    for cp in outs:
        cp.wait()


def local(ntx, nty, state, courant, diffusion, conv_mask, w_in, w_hidden, w_out):
    lon, lat, ch = state.shape
    cols = lon * lat
    hid = w_in.shape[1]
    wide = GRP * lat
    chunks = cols // wide
    vmem = pl.BlockSpec(memory_space=pltpu.VMEM)
    hbm = pl.BlockSpec(memory_space=pltpu.MemorySpace.HBM)
    adv, w_in, w_hidden, w_out = pl.pallas_call(
        functools.partial(advance_kernel, ntx, nty),
        out_shape=[
            pltpu.VMEM((lon, lat, ch), jnp.float32),
            pltpu.VMEM(w_in.shape, jnp.bfloat16),
            pltpu.VMEM(w_hidden.shape, jnp.bfloat16),
            pltpu.VMEM(w_out.shape, jnp.bfloat16),
        ],
        in_specs=[hbm, hbm, vmem, hbm, hbm, hbm],
        out_specs=[vmem] * 4,
        scratch_shapes=[
            pltpu.VMEM((lon + 2, lat + 2 * PAD, ch), jnp.float32),
            pltpu.VMEM((lon, lat, ch), jnp.bfloat16),
            pltpu.VMEM((lon, 1, ch), jnp.float32),
            pltpu.VMEM((lon, 1, ch), jnp.float32),
            pltpu.VMEM((1, lat, ch), jnp.float32),
            pltpu.VMEM((1, lat, ch), jnp.float32),
            pltpu.VMEM((lon, 8, ch), jnp.float32),
            pltpu.VMEM((lon, 8, ch), jnp.float32),
            pltpu.SemaphoreType.DMA((PIECES,)),
            pltpu.SemaphoreType.DMA((PIECES,)),
            pltpu.SemaphoreType.DMA((3,)),
            pltpu.SemaphoreType.DMA((4,)),
            pltpu.SemaphoreType.DMA((4,)),
        ],
        compiler_params=pltpu.CompilerParams(collective_id=0, has_side_effects=True,
                                             vmem_limit_bytes=ROOM),
        name="advance",
    )(state, courant, diffusion.T, w_in, w_hidden, w_out)
    out = pl.pallas_call(
        closure_kernel,
        out_shape=jax.ShapeDtypeStruct((cols, ch), jnp.float32),
        in_specs=[vmem] * 5,
        out_specs=hbm,
        scratch_shapes=[
            pltpu.VMEM((cols, ch), jnp.float32),
            pltpu.VMEM((cols // 2 + wide + 32, ch), jnp.bfloat16),
            pltpu.VMEM((TM, hid), jnp.bfloat16),
            pltpu.VMEM((TM, hid), jnp.bfloat16),
            pltpu.VMEM((chunks, wide), jnp.float32),
            pltpu.VMEM((chunks, 128), jnp.int32),
            pltpu.SMEM((chunks, 128), jnp.int32),
            pltpu.SemaphoreType.DMA,
            pltpu.SemaphoreType.DMA((chunks,)),
        ],
        compiler_params=pltpu.CompilerParams(vmem_limit_bytes=ROOM // 2),
        name="closure",
    )(conv_mask.T, adv, w_in, w_hidden, w_out)
    return out.reshape(lon, lat, ch)


def solution(mesh):
    spec = P(("member", "tx"), "ty", None)
    flat = P(("member", "tx"), "ty")
    return jax.shard_map(
        functools.partial(local, mesh.shape["tx"], mesh.shape["ty"]),
        mesh=mesh,
        in_specs=(spec, spec, flat, flat, P(), P(), P()),
        out_specs=spec,
        check_vma=False,
    )
```
